128 devices in a mesh: dp: 8 (over z, core), expert: 16 (over y, x).
Axes of the slice: x: 4, y: 4, z: 4, core: 2. Of those that a mesh axis runs over, the one named last changes fastest.
Arguments:
- tokens: bfloat16 [16384, 4096], P(('dp', 'expert')), may hold values from -6 to 6
- cotangent: bfloat16 [16384, 4096], P(('dp', 'expert')), may hold values from -0.796875 to 0.796875
- router_probs: float32 [16384, 4], P(('dp', 'expert')), may hold values from 0.1 to 1
- routing: int32 [16384, 4], P(('dp', 'expert')), may hold values from 0 to 127, all different within a row
- hot_marks: int32 [128], replicated, may hold values from 0 to 1, as said below
- cap_counts: int32 [128], replicated, may hold values from 2 to 4, as said below
- gate_up: bfloat16 [128, 2, 4096, 768], P(('dp', 'expert')), may hold values from -0.09375 to 0.09375
- adapter_in: bfloat16 [128, 32, 768], P(('dp', 'expert')), may hold values from -0.21875 to 0.21875
- adapter_out: bfloat16 [128, 32, 4096], P(('dp', 'expert')), may hold values from -0.09375 to 0.09375
Outputs:
- in_gradient: float32 [128, 32, 768], P(('dp', 'expert'))
- out_gradient: float32 [128, 32, 4096], P(('dp', 'expert'))
The draws below stay inside these ranges and needn't reach their ends.
Inputs may be any that keep to these rules, and one draw needn't show every extreme that they name: `routing`: each token names 4 different experts. `hot_marks`: of every two experts whose numbers differ only in the bit of value 16 / 2, exactly one is marked. `cap_counts`: some expert's count equals 4.
All inputs are finite; a program needn't handle non-finite values.
Results may differ from the reference program's by a relative error of at most 0.005.
Values may be sent and summed in bfloat16 or wider, within the bound.
No kernel may reach another device: no remote copies, remote signals or barrier semaphores. Data moves between devices by JAX's collectives and lax.ppermute only.
A program may use at most 192 MiB of HBM per device.

```python
import jax
import jax.numpy as jnp
from jax import lax

D = 4096
FF = 768
RANK = 32
TOPK = 4
TOK_DEV = 128
EXPERTS = 128
TOKENS = 16384
CAP = 4
N_EXPERT = 16
DEVICES = 128


def draw_hot_marks(key, part):
    expert_ids = jnp.arange(EXPERTS, dtype=jnp.int32)
    coins = jax.random.randint(key, (EXPERTS,), 0, 2).astype(jnp.int32)
    partner = jnp.bitwise_xor(expert_ids, N_EXPERT // 2)
    lower_half = expert_ids % N_EXPERT < N_EXPERT // 2
    return jnp.where(lower_half, coins, 1 - coins[partner]).astype(jnp.int32)


def draw_cap_counts(key, part):
    lowest = (CAP + 1) // 2
    values = jax.random.randint(key, (EXPERTS,), lowest, CAP + 1).astype(jnp.int32)
    filled = jax.random.randint(jax.random.fold_in(key, 7), (EXPERTS,), 0, 4) == 0
    values = jnp.where(filled, CAP, values)
    chosen = jax.random.randint(jax.random.fold_in(key, 11), (), 0, EXPERTS)
    return values.at[chosen].set(CAP).astype(jnp.int32)


def steps_of(stream_key, shape, cuts, smallest, high):
    level, own = 1.0, jax.random.fold_in(stream_key, 6)
    for position, blocks in cuts:
        heights = jnp.exp(jax.random.uniform(jax.random.fold_in(own, position), (blocks,), jnp.float32, smallest / len(cuts), high / len(cuts)))
        level = level * jnp.repeat(heights, shape[position] // blocks).reshape([-1 if axis == position else 1 for axis in range(len(shape))])
    return level


def different_ones(stream_key, rows, count, top, lift):
    order = jax.random.permutation(jax.random.fold_in(stream_key, 1), count)
    pull = order
    for power in range(3):
        pull = pull * pull // count
    pull = pull * lift // count
    lots = jax.random.randint(jax.random.fold_in(stream_key, 2), (rows, count), 0, 4096) + pull
    sure = jax.random.permutation(jax.random.fold_in(stream_key, 3), rows)[jnp.arange(count) % rows]
    lots = jnp.where(jnp.arange(rows)[:, None] == sure[None, :], 1 << 14, lots)
    priority = lots * count + jnp.arange(count)
    return lax.top_k(priority.astype(jnp.int32), top)[1].astype(jnp.int32)


def gaussian(rng, shape, width, reach, split=(), kind=jnp.bfloat16):
    entries = jax.random.normal(rng, shape, jnp.float32) * width
    if len(split) > 0:
        entries = steps_of(rng, shape, split, -0.22, 0.18) * entries
    return jnp.clip(entries, min=-reach, max=reach).astype(kind)


def setup_inputs(seed: int = 0) -> dict:
    streams_of = jax.random.split(jax.random.key(seed), 10)
    return {
        "tokens": gaussian(streams_of[0], (TOKENS, D), 1.0, 6.0, ((0, 128),)),
        "cotangent": gaussian(streams_of[1], (TOKENS, D), 0.1, 0.796875, ((0, 128),)),
        "router_probs": jnp.clip(0.1 + 0.9 * jax.random.uniform(streams_of[2], (TOKENS, TOPK), jnp.float32) ** steps_of(streams_of[2], (TOKENS, TOPK), ((0, 128),), -0.2, 0.2), 0.1, 1.0),
        "routing": different_ones(streams_of[3], TOKENS, EXPERTS, TOPK, 512),
        "hot_marks": draw_hot_marks(jax.random.fold_in(streams_of[9], 71), 0),
        "cap_counts": draw_cap_counts(jax.random.fold_in(streams_of[9], 71), 0),
        "gate_up": gaussian(streams_of[6], (EXPERTS, 2, D, FF), D ** -0.5, 0.09375, ((0, 128),)),
        "adapter_in": gaussian(streams_of[7], (EXPERTS, RANK, FF), FF ** -0.5, 0.21875, ((0, 128),)),
        "adapter_out": gaussian(streams_of[8], (EXPERTS, RANK, D), D ** -0.5, 0.09375, ((0, 128),)),
    }


adapter_scale_factor = 2.0


def reference(tokens, cotangent, router_probs, routing, hot_marks, cap_counts, gate_up, adapter_in, adapter_out):
    pair_count = TOK_DEV * TOPK
    flat_route = routing.reshape(DEVICES, pair_count)
    expert_ids = jnp.arange(EXPERTS, dtype=jnp.int32)

    def rank_block(route_row):
        onehot = (route_row[:, None] == expert_ids[None, :]).astype(jnp.int32)
        return jnp.sum((jnp.cumsum(onehot, axis=0) - onehot) * onehot, axis=1)

    order_rank = lax.map(rank_block, flat_route)
    limit_rows = cap_counts + CAP * hot_marks
    kept_mask = order_rank < limit_rows[flat_route]
    slot_width = 2 * CAP
    source = jnp.broadcast_to(jnp.arange(DEVICES, dtype=jnp.int32)[:, None], flat_route.shape)
    pair_ids = jnp.arange(DEVICES * pair_count, dtype=jnp.int32).reshape(DEVICES, pair_count)
    column = jnp.where(kept_mask, order_rank, slot_width).astype(jnp.int32)
    slot_table = jnp.full((DEVICES, EXPERTS, slot_width + 1), -1, jnp.int32)
    slot_table = slot_table.at[source, flat_route, column].set(pair_ids)[:, :, :slot_width]
    probs_flat = router_probs.reshape(-1)

    def one_expert(expert):
        chosen = lax.dynamic_index_in_dim(slot_table, expert, 1, keepdims=False).reshape(-1)
        valid_rows = chosen >= 0
        safe_ids = jnp.maximum(chosen, 0)
        token_ids = safe_ids // TOPK
        inputs = tokens[token_ids]
        factor = jnp.where(valid_rows, probs_flat[safe_ids], 0.0)
        scaled_adapter_output = (factor[:, None] * cotangent[token_ids].astype(jnp.float32)).astype(jnp.bfloat16)
        weights = lax.dynamic_index_in_dim(gate_up, expert, 0, keepdims=False)
        gate_out = jnp.dot(inputs, weights[0], preferred_element_type=jnp.float32)
        up_out = jnp.dot(inputs, weights[1], preferred_element_type=jnp.float32)
        hidden_state_rows = (jax.nn.silu(gate_out) * up_out).astype(jnp.bfloat16)
        adapter_down_matrix = lax.dynamic_index_in_dim(adapter_in, expert, 0, keepdims=False)
        adapter_up_matrix = lax.dynamic_index_in_dim(adapter_out, expert, 0, keepdims=False)
        rank_projected_rows = (adapter_scale_factor * jnp.dot(hidden_state_rows, adapter_down_matrix.T, preferred_element_type=jnp.float32)).astype(jnp.bfloat16)
        rank_gradient_rows = (adapter_scale_factor * jnp.dot(scaled_adapter_output, adapter_up_matrix.T, preferred_element_type=jnp.float32)).astype(jnp.bfloat16)
        grad_first = jnp.dot(rank_gradient_rows.T, hidden_state_rows, preferred_element_type=jnp.float32)
        grad_second = jnp.dot(rank_projected_rows.T, scaled_adapter_output, preferred_element_type=jnp.float32)
        return grad_first, grad_second

    in_gradient, out_gradient = lax.map(one_expert, expert_ids)
    return in_gradient, out_gradient
```

```python
import jax
import jax.numpy as jnp
from jax import lax
from jax.sharding import PartitionSpec as P

SCALE = 2.0
SLOTS = 8
AXES = ("dp", "expert")


def slot_masks(routing, router_probs, hot_marks, cap_counts):
    tok_count, top_count = routing.shape
    experts = cap_counts.shape[0]
    expert_ids = jnp.arange(experts, dtype=jnp.int32)
    limit = cap_counts + (tok_count * top_count // experts) * hot_marks
    hit = routing.T[:, None, :] == expert_ids[None, :, None]
    member = jnp.any(hit, axis=0)
    weight = jnp.sum(jnp.where(hit, router_probs.T[:, None, :], 0.0), axis=0)
    before = lax.broadcasted_iota(jnp.int32, (tok_count, tok_count), 0) < lax.broadcasted_iota(
        jnp.int32, (tok_count, tok_count), 1
    )
    rank = jnp.dot(
        member.astype(jnp.bfloat16), before.astype(jnp.bfloat16), preferred_element_type=jnp.float32
    ).astype(jnp.int32)
    rank = jnp.where(member & (rank < limit[:, None]), rank, -1)
    slots = lax.broadcasted_iota(jnp.int32, (experts, SLOTS, tok_count), 1)
    sel = rank[:, None, :] == slots
    factor = jnp.sum(jnp.where(sel, weight[:, None, :], 0.0), axis=2)
    return sel, factor


def body(
    tokens, cotangent, router_probs, routing, hot_marks, cap_counts, gate_up, adapter_in, adapter_out
):
    tok_count, model_width = tokens.shape
    experts = cap_counts.shape[0]
    rows = experts * SLOTS
    sel, factor = slot_masks(routing, router_probs, hot_marks, cap_counts)
    pick = sel.reshape(rows, tok_count).astype(jnp.bfloat16)
    sent_tokens = jnp.dot(pick, tokens, preferred_element_type=jnp.float32).astype(jnp.bfloat16)
    inputs = lax.all_to_all(
        sent_tokens.reshape(experts, SLOTS, model_width), AXES, split_axis=0, concat_axis=0, tiled=True
    ).reshape(rows, model_width)
    picked = jnp.dot(pick, cotangent, preferred_element_type=jnp.float32)
    sent_scaled = (factor.reshape(rows, 1) * picked).astype(jnp.bfloat16)
    scaled = lax.all_to_all(
        sent_scaled.reshape(experts, SLOTS, model_width), AXES, split_axis=0, concat_axis=0, tiled=True
    ).reshape(rows, model_width)
    gate_out = jnp.dot(inputs, gate_up[0, 0], preferred_element_type=jnp.float32)
    up_out = jnp.dot(inputs, gate_up[0, 1], preferred_element_type=jnp.float32)
    hidden = (jax.nn.silu(gate_out) * up_out).astype(jnp.bfloat16)
    low = (
        SCALE * jnp.einsum("nf,rf->nr", hidden, adapter_in[0], preferred_element_type=jnp.float32)
    ).astype(jnp.bfloat16)
    back = (
        SCALE * jnp.einsum("nd,rd->nr", scaled, adapter_out[0], preferred_element_type=jnp.float32)
    ).astype(jnp.bfloat16)
    in_grad = jnp.einsum("nr,nf->rf", back, hidden, preferred_element_type=jnp.float32)
    out_grad = jnp.einsum("nr,nd->rd", low, scaled, preferred_element_type=jnp.float32)
    return in_grad[None], out_grad[None]


def solution(mesh):
    in_specs = (
        P(AXES, None),
        P(AXES, None),
        P(AXES, None),
        P(AXES, None),
        P(),
        P(),
        P(AXES, None, None, None),
        P(AXES, None, None),
        P(AXES, None, None),
    )
    out_specs = (P(AXES, None, None), P(AXES, None, None))
    return jax.shard_map(body, mesh=mesh, in_specs=in_specs, out_specs=out_specs, check_vma=False)
```

```python
import functools

import jax
import jax.numpy as jnp
from jax import lax
from jax.experimental import pallas as pl
from jax.experimental.pallas import tpu as pltpu
from jax.sharding import PartitionSpec as P


SCALE = 2.0
SLOTS = 8
BASE = 4
EXTRA = 2
GROUP = 16
AXES = ("dp", "expert")


def slot_table(experts, routing, probs, limit):
    tok_count = routing.shape[1]
    hit = [routing[k : k + 1, :] == experts for k in range(routing.shape[0])]
    member = sum(jnp.where(h, 1.0, 0.0) for h in hit)
    weight = sum(jnp.where(h, probs[k : k + 1, :], 0.0) for k, h in enumerate(hit))
    before = lax.broadcasted_iota(jnp.int32, (tok_count, tok_count), 0) < lax.broadcasted_iota(
        jnp.int32, (tok_count, tok_count), 1
    )
    rank = jnp.dot(
        member.astype(jnp.bfloat16),
        jnp.where(before, 1.0, 0.0).astype(jnp.bfloat16),
        preferred_element_type=jnp.float32,
    ).astype(jnp.int32)
    return jnp.where((member > 0.0) & (rank < limit), rank, -1), weight


def look_up(table, experts):
    lanes = lax.broadcasted_iota(jnp.int32, (experts.shape[0], table.shape[1]), 1)
    return jnp.sum(jnp.where(lanes == experts, table, 0), axis=1, keepdims=True)


def block_experts():
    first = pl.program_id(0) * GROUP
    return first + lax.broadcasted_iota(jnp.int32, (GROUP, 1), 0)


def spread(rank, weight, rows, parts):
    group, tok_count = rank.shape
    sublane = lax.broadcasted_iota(jnp.int32, (group, SLOTS, tok_count), 1)
    match = rank[:, None, :] == sublane // parts
    factor = jnp.sum(jnp.where(match, weight[:, None, :], 0.0), axis=2, keepdims=True)
    width = rows.shape[1] // parts
    total = jnp.zeros((group * SLOTS, width), jnp.float32)
    for part in range(parts):
        pick = jnp.where(match & (sublane % parts == part), 1.0, 0.0).astype(jnp.bfloat16)
        total += jnp.dot(
            pick.reshape(group * SLOTS, tok_count),
            rows[:, part * width : (part + 1) * width],
            preferred_element_type=jnp.float32,
        )
    return (total.reshape(group, SLOTS, width) * factor).astype(jnp.bfloat16)


def pack_first_kernel(half, room, routing, probs, marks, caps, tokens, cotangent, out):
    tok_count, width = tokens.shape
    experts = block_experts()
    marked = look_up(marks[...], experts)
    limit = look_up(caps[...], experts) + room * marked
    rank, _ = slot_table(experts, routing[...], probs[...], limit)
    sublane = lax.broadcasted_iota(jnp.int32, (GROUP, SLOTS, tok_count), 1)
    pick = jnp.where(rank[:, None, :] == sublane, 1.0, 0.0).astype(jnp.bfloat16)
    rows = jnp.dot(
        pick.reshape(GROUP * SLOTS, tok_count), tokens[...], preferred_element_type=jnp.float32
    )
    out[:, :, :width] = rows.astype(jnp.bfloat16).reshape(GROUP, SLOTS, width)
    hot = jnp.where(marked == 1, experts, experts ^ half)
    hot_rank, hot_weight = slot_table(
        hot, routing[...], probs[...], look_up(caps[...], hot) + room
    )
    hot_rank = hot_rank - jnp.where(marked == 1, BASE, BASE + EXTRA)
    out[:, :, width:] = spread(hot_rank, hot_weight, cotangent, SLOTS // EXTRA)


def pack_second_kernel(room, routing, probs, marks, caps, cotangent, out):
    experts = block_experts()
    limit = look_up(caps[...], experts) + room * look_up(marks[...], experts)
    rank, weight = slot_table(experts, routing[...], probs[...], limit)
    out[...] = spread(rank, weight, cotangent, SLOTS // BASE)


def pack(kernel, tables, arrays, width):
    experts = tables[-1].shape[1]
    operands = tables + arrays
    return pl.pallas_call(
        kernel,
        grid=(experts // GROUP,),
        in_specs=[pl.BlockSpec(x.shape, lambda i: (0, 0)) for x in operands],
        out_specs=pl.BlockSpec((GROUP, SLOTS, width), lambda i: (i, 0, 0)),
        out_shape=jax.ShapeDtypeStruct((experts, SLOTS, width), jnp.bfloat16),
    )(*operands)


def finish_kernel(base, low, hidden, own_out, grad, in_grad):
    step = pl.program_id(0)
    block, width = base.shape
    parts = SLOTS // BASE
    row = lax.broadcasted_iota(jnp.int32, (block, block), 0)
    column = lax.broadcasted_iota(jnp.int32, (block, block), 1)
    same = row // SLOTS == column // SLOTS
    widen = jnp.where(same & (row % SLOTS // parts == column % SLOTS), 1.0, 0.0).astype(low.dtype)
    narrow = jnp.where(same & (row % SLOTS * parts == column % SLOTS), 1.0, 0.0).astype(low.dtype)
    rows_low = jnp.dot(widen, low[...], preferred_element_type=jnp.float32).astype(low.dtype)
    part = lax.broadcasted_iota(jnp.int32, rows_low.shape, 0) % parts
    back = None
    for at in range(parts):
        columns = slice(at * width, (at + 1) * width)
        part_low = jnp.where(part == at, rows_low, jnp.zeros((), low.dtype))
        new = lax.dot_general(
            part_low, base[...], (((0,), (0,)), ((), ())), preferred_element_type=jnp.float32
        )
        grad[:, columns] = jnp.where(step == 0, 0.0, grad[:, columns]) + new
        half_back = lax.dot_general(
            base[...], own_out[:, columns], (((1,), (1,)), ((), ())), preferred_element_type=jnp.float32
        )
        back = half_back if back is None else back + pltpu.roll(half_back, block - at, 0)
    back = (SCALE * back).astype(jnp.bfloat16)
    back = jnp.dot(narrow, back, preferred_element_type=jnp.float32).astype(jnp.bfloat16)
    new_in = lax.dot_general(
        back, hidden[...], (((0,), (0,)), ((), ())), preferred_element_type=jnp.float32
    )
    in_grad[...] = jnp.where(step == 0, 0.0, in_grad[...]) + new_in


def finish(base, low, hidden, own_out):
    rows, width = base.shape
    rank_width, hidden_width = low.shape[1], hidden.shape[1]
    block = rows // 4
    row_block = lambda columns: pl.BlockSpec((block, columns), lambda i: (i, 0))
    kept = lambda shape: pl.BlockSpec(shape, lambda i: (0, 0))
    return pl.pallas_call(
        finish_kernel,
        grid=(rows // block,),
        in_specs=[row_block(width), row_block(rank_width), row_block(hidden_width), kept(own_out.shape)],
        out_specs=[kept(own_out.shape), kept((rank_width, hidden_width))],
        out_shape=[
            jax.ShapeDtypeStruct(own_out.shape, jnp.float32),
            jax.ShapeDtypeStruct((rank_width, hidden_width), jnp.float32),
        ],
    )(base, low, hidden, own_out)


def exchange(block):
    return lax.all_to_all(block, AXES, split_axis=0, concat_axis=0, tiled=True)


def layer(
    tokens, cotangent, router_probs, routing, hot_marks, cap_counts, gate_up, adapter_in, adapter_out
):
    model_width = tokens.shape[1]
    experts = cap_counts.shape[0]
    n_expert = lax.axis_size("expert")
    half = n_expert // 2
    pairs = [(i, i ^ half) for i in range(n_expert)]
    own_index = lax.axis_index("dp") * n_expert + lax.axis_index("expert")
    own_marked = lax.dynamic_index_in_dim(hot_marks, own_index, 0, keepdims=False) == 1
    own_in, own_out = adapter_in[0], adapter_out[0]

    partner_out = lax.ppermute(own_out, "expert", pairs)
    room = tokens.shape[0] * routing.shape[1] // experts
    tables = (routing.T, router_probs.T, hot_marks[None, :], cap_counts[None, :])
    first = pack(
        functools.partial(pack_first_kernel, half, room),
        tables,
        (tokens, cotangent),
        model_width + EXTRA * model_width // SLOTS,
    )
    first = exchange(first)
    second = pack(
        functools.partial(pack_second_kernel, room), tables, (cotangent,), BASE * model_width // SLOTS
    )
    second = exchange(second)

    inputs = first[:, :, :model_width].reshape(experts * SLOTS, model_width)
    gate_out = jnp.dot(inputs, gate_up[0, 0], preferred_element_type=jnp.float32)
    up_out = jnp.dot(inputs, gate_up[0, 1], preferred_element_type=jnp.float32)
    hidden = (jax.nn.silu(gate_out) * up_out).astype(jnp.bfloat16)
    low = (
        SCALE * jnp.einsum("nf,rf->nr", hidden, own_in, preferred_element_type=jnp.float32)
    ).astype(jnp.bfloat16)
    rank_width, hidden_width = own_in.shape
    hidden = hidden.reshape(experts, SLOTS, hidden_width)
    low = low.reshape(experts, SLOTS, rank_width)

    parts = SLOTS // EXTRA
    extra = first[:, :, model_width:].reshape(experts, EXTRA, parts, model_width // parts)
    extra = extra.reshape(experts * EXTRA, model_width)
    work_out = jnp.where(own_marked, own_out, partner_out)
    extra_back = (
        SCALE * jnp.einsum("nd,rd->nr", extra, work_out, preferred_element_type=jnp.float32)
    ).astype(jnp.bfloat16)
    extra_back = extra_back.reshape(experts, EXTRA, rank_width)
    swapped = lax.ppermute(
        jnp.where(own_marked, low[:, BASE + EXTRA :], extra_back), "expert", pairs
    )
    extra_low = jnp.where(own_marked, low[:, BASE : BASE + EXTRA], swapped)
    extra_grad = jnp.einsum(
        "nr,nd->rd",
        extra_low.reshape(experts * EXTRA, rank_width),
        extra,
        preferred_element_type=jnp.float32,
    )
    returned = lax.ppermute(extra_grad, "expert", pairs)
    hot_back = jnp.concatenate([extra_back, swapped], axis=1)
    hot_back = jnp.where(own_marked, hot_back, jnp.zeros((), jnp.bfloat16))
    in_grad = jnp.einsum(
        "sjr,sjf->rf", hot_back, hidden[:, BASE:], preferred_element_type=jnp.float32
    )

    base_grad, base_in = finish(
        second.reshape(experts * SLOTS, BASE * model_width // SLOTS),
        low.reshape(experts * SLOTS, rank_width),
        hidden.reshape(experts * SLOTS, hidden_width),
        own_out,
    )
    in_grad = base_in + in_grad
    out_grad = base_grad + jnp.where(own_marked, extra_grad + returned, 0.0)
    return in_grad[None], out_grad[None]


def solution(mesh):
    in_specs = (
        P(AXES, None),
        P(AXES, None),
        P(AXES, None),
        P(AXES, None),
        P(),
        P(),
        P(AXES, None, None, None),
        P(AXES, None, None),
        P(AXES, None, None),
    )
    out_specs = (P(AXES, None, None), P(AXES, None, None))
    return jax.shard_map(layer, mesh=mesh, in_specs=in_specs, out_specs=out_specs, check_vma=False)
```

```python
import functools

import jax
import jax.numpy as jnp
from jax import lax
from jax.experimental import pallas as pl
from jax.experimental.pallas import tpu as pltpu
from jax.sharding import PartitionSpec as P


SCALE = 2.0
SLOTS = 8
BASE = 4
EXTRA = 2
GROUP = 16
AXES = ("dp", "expert")


def slot_table(experts, routing, probs, limit):
    tok_count = routing.shape[1]
    hit = [routing[k : k + 1, :] == experts for k in range(routing.shape[0])]
    member = sum(jnp.where(h, 1.0, 0.0) for h in hit)
    weight = sum(jnp.where(h, probs[k : k + 1, :], 0.0) for k, h in enumerate(hit))
    before = lax.broadcasted_iota(jnp.int32, (tok_count, tok_count), 0) < lax.broadcasted_iota(
        jnp.int32, (tok_count, tok_count), 1
    )
    rank = jnp.dot(
        member.astype(jnp.bfloat16),
        jnp.where(before, 1.0, 0.0).astype(jnp.bfloat16),
        preferred_element_type=jnp.float32,
    ).astype(jnp.int32)
    return jnp.where((member > 0.0) & (rank < limit), rank, -1), weight


def look_up(table, experts):
    lanes = lax.broadcasted_iota(jnp.int32, (experts.shape[0], table.shape[1]), 1)
    return jnp.sum(jnp.where(lanes == experts, table, 0), axis=1, keepdims=True)


def block_experts():
    first = pl.program_id(0) * GROUP
    return first + lax.broadcasted_iota(jnp.int32, (GROUP, 1), 0)


def spread(rank, weight, rows, parts):
    group, tok_count = rank.shape
    sublane = lax.broadcasted_iota(jnp.int32, (group, SLOTS, tok_count), 1)
    match = rank[:, None, :] == sublane // parts
    factor = jnp.sum(jnp.where(match, weight[:, None, :], 0.0), axis=2, keepdims=True)
    width = rows.shape[1] // parts
    total = jnp.zeros((group * SLOTS, width), jnp.float32)
    for part in range(parts):
        pick = jnp.where(match & (sublane % parts == part), 1.0, 0.0).astype(jnp.bfloat16)
        total += jnp.dot(
            pick.reshape(group * SLOTS, tok_count),
            rows[:, part * width : (part + 1) * width],
            preferred_element_type=jnp.float32,
        )
    return (total.reshape(group, SLOTS, width) * factor).astype(jnp.bfloat16)


def pack_kernel(half, room, routing, probs, marks, caps, own, tokens, cotangent, first, second):
    tok_count, width = tokens.shape
    experts = block_experts()
    marked = look_up(marks[...], experts)
    limit = look_up(caps[...], experts) + room * marked
    rank, weight = slot_table(experts, routing[...], probs[...], limit)
    sublane = lax.broadcasted_iota(jnp.int32, (GROUP, SLOTS, tok_count), 1)
    pick = jnp.where(rank[:, None, :] == sublane, 1.0, 0.0).astype(jnp.bfloat16)
    rows = jnp.dot(
        pick.reshape(GROUP * SLOTS, tok_count), tokens[...], preferred_element_type=jnp.float32
    )
    first[:, :, :width] = rows.reshape(GROUP, SLOTS, width).astype(jnp.bfloat16)
    hot = jnp.where(marked == 1, experts, experts ^ half)
    hot_rank, hot_weight = slot_table(
        hot, routing[...], probs[...], look_up(caps[...], hot) + room
    )
    hot_rank = hot_rank - jnp.where(marked == 1, BASE, BASE + EXTRA)
    first[:, :, width:] = spread(hot_rank, hot_weight, cotangent, SLOTS // EXTRA)
    second[...] = spread(rank, weight, cotangent, SLOTS // BASE)


def pack(half, room, tables, arrays):
    experts = tables[2].shape[1]
    model_width = arrays[0].shape[1]
    operands = tables + arrays
    widths = (model_width + EXTRA * model_width // SLOTS, BASE * model_width // SLOTS)
    return pl.pallas_call(
        functools.partial(pack_kernel, half, room),
        grid=(experts // GROUP,),
        in_specs=[pl.BlockSpec(x.shape, lambda i: (0, 0)) for x in operands],
        out_specs=[pl.BlockSpec((GROUP, SLOTS, w), lambda i: (i, 0, 0)) for w in widths],
        out_shape=[jax.ShapeDtypeStruct((experts, SLOTS, w), jnp.bfloat16) for w in widths],
    )(*operands)


def finish_kernel(base, low, hidden, wide_out, grad_start, in_start, grad, in_grad, total):
    step = pl.program_id(0)
    block, width = base.shape
    parts, rank_width = SLOTS // BASE, grad.shape[0]
    row = lax.broadcasted_iota(jnp.int32, (block, block), 0)
    column = lax.broadcasted_iota(jnp.int32, (block, block), 1)
    same = row // SLOTS == column // SLOTS
    widen = jnp.where(same & (row % SLOTS // parts == column % SLOTS), 1.0, 0.0).astype(low.dtype)
    narrow = jnp.where(same & (row % SLOTS * parts == column % SLOTS), 1.0, 0.0).astype(low.dtype)
    rows_low = jnp.dot(
        widen, jnp.tile(low[...], (1, parts)), preferred_element_type=jnp.float32
    )
    part = lax.broadcasted_iota(jnp.int32, rows_low.shape, 0) % parts
    own = part == lax.broadcasted_iota(jnp.int32, rows_low.shape, 1) // rank_width
    wide_low = jnp.where(own, rows_low, 0.0).astype(low.dtype)
    new = lax.dot_general(
        wide_low, base[...], (((0,), (0,)), ((), ())), preferred_element_type=jnp.float32
    )
    halves = lax.dot_general(
        base[...], wide_out[...], (((1,), (1,)), ((), ())), preferred_element_type=jnp.float32
    )
    back = halves[:, :rank_width]
    for at in range(1, parts):
        later = halves[:, at * rank_width : (at + 1) * rank_width]
        back = back + pltpu.roll(later, block - at, 0)
    back = (SCALE * back).astype(jnp.bfloat16)
    back = jnp.dot(narrow, back, preferred_element_type=jnp.float32).astype(jnp.bfloat16)
    new_in = lax.dot_general(
        back, hidden[...], (((0,), (0,)), ((), ())), preferred_element_type=jnp.float32
    )

    @pl.when(step == 0)
    def _():
        total[...] = new
        in_grad[...] = in_start[...] + new_in

    @pl.when(step > 0)
    def _():
        total[...] += new
        in_grad[...] += new_in

    @pl.when(step == pl.num_programs(0) - 1)
    def _():
        for at in range(parts):
            columns = slice(at * width, (at + 1) * width)
            rows = slice(at * rank_width, (at + 1) * rank_width)
            grad[:, columns] = grad_start[:, columns] + total[rows, :]


def finish(base, low, hidden, wide_out, grad_start, in_start):
    rows, width = base.shape
    rank_width, hidden_width = low.shape[1], hidden.shape[1]
    block = rows // 4
    row_block = lambda columns: pl.BlockSpec((block, columns), lambda i: (i, 0))
    kept = lambda array: pl.BlockSpec(array.shape, lambda i: (0, 0))
    return pl.pallas_call(
        finish_kernel,
        grid=(rows // block,),
        in_specs=[row_block(width), row_block(rank_width), row_block(hidden_width)]
        + [kept(wide_out), kept(grad_start), kept(in_start)],
        out_specs=[kept(grad_start), kept(in_start)],
        out_shape=[
            jax.ShapeDtypeStruct(grad_start.shape, jnp.float32),
            jax.ShapeDtypeStruct(in_start.shape, jnp.float32),
        ],
        scratch_shapes=[pltpu.VMEM((SLOTS // BASE * rank_width, width), jnp.float32)],
    )(base, low, hidden, wide_out, grad_start, in_start)


def exchange(block):
    return lax.all_to_all(block, AXES, split_axis=0, concat_axis=0, tiled=True)


def layer(
    tokens, cotangent, router_probs, routing, hot_marks, cap_counts, gate_up, adapter_in, adapter_out
):
    model_width = tokens.shape[1]
    experts = cap_counts.shape[0]
    n_expert = lax.axis_size("expert")
    half = n_expert // 2
    pairs = [(i, i ^ half) for i in range(n_expert)]
    own_index = lax.axis_index("dp") * n_expert + lax.axis_index("expert")
    own_marked = lax.dynamic_index_in_dim(hot_marks, own_index, 0, keepdims=False) == 1
    own_in, own_out = adapter_in[0], adapter_out[0]

    partner_out = lax.ppermute(own_out, "expert", pairs)
    room = tokens.shape[0] * routing.shape[1] // experts
    tables = (
        routing.T,
        router_probs.T,
        hot_marks[None, :],
        cap_counts[None, :],
        own_marked.astype(jnp.int32).reshape(1, 1),
    )
    first, second = pack(half, room, tables, (tokens, cotangent))
    first = exchange(first)
    second = exchange(second)

    inputs = first[:, :, :model_width].reshape(experts * SLOTS, model_width)
    gate_out = jnp.dot(inputs, gate_up[0, 0], preferred_element_type=jnp.float32)
    up_out = jnp.dot(inputs, gate_up[0, 1], preferred_element_type=jnp.float32)
    hidden = (jax.nn.silu(gate_out) * up_out).astype(jnp.bfloat16)
    low = (
        SCALE * jnp.einsum("nf,rf->nr", hidden, own_in, preferred_element_type=jnp.float32)
    ).astype(jnp.bfloat16)
    rank_width, hidden_width = own_in.shape
    hidden = hidden.reshape(experts, SLOTS, hidden_width)
    low = low.reshape(experts, SLOTS, rank_width)

    parts = SLOTS // EXTRA
    extra = first[:, :, model_width:].reshape(experts, EXTRA, parts, model_width // parts)
    extra = extra.reshape(experts * EXTRA, model_width)
    work_out = jnp.where(own_marked, own_out, partner_out)
    extra_back = (
        SCALE * jnp.einsum("nd,rd->nr", extra, work_out, preferred_element_type=jnp.float32)
    ).astype(jnp.bfloat16)
    extra_back = extra_back.reshape(experts, EXTRA, rank_width)
    swapped = lax.ppermute(
        jnp.where(own_marked, low[:, BASE + EXTRA :], extra_back), "expert", pairs
    )
    extra_low = jnp.where(own_marked, low[:, BASE : BASE + EXTRA], swapped)
    extra_grad = jnp.einsum(
        "nr,nd->rd",
        extra_low.reshape(experts * EXTRA, rank_width),
        extra,
        preferred_element_type=jnp.float32,
    )
    returned = lax.ppermute(extra_grad, "expert", pairs)
    hot_back = jnp.concatenate([extra_back, swapped], axis=1)
    hot_back = jnp.where(own_marked, hot_back, jnp.zeros((), jnp.bfloat16))
    in_grad = jnp.einsum(
        "sjr,sjf->rf", hot_back, hidden[:, BASE:], preferred_element_type=jnp.float32
    )

    parts, width = SLOTS // BASE, BASE * model_width // SLOTS
    wide_out = jnp.concatenate(
        [own_out[:, at * width : (at + 1) * width] for at in range(parts)], axis=0
    )
    grad, in_grad = finish(
        second.reshape(experts * SLOTS, width),
        low.reshape(experts * SLOTS, rank_width),
        hidden.reshape(experts * SLOTS, hidden_width),
        wide_out,
        jnp.where(own_marked, extra_grad, 0.0),
        in_grad,
    )
    out_grad = grad + jnp.where(own_marked, returned, 0.0)
    return in_grad[None], out_grad[None]


def solution(mesh):
    in_specs = (
        P(AXES, None),
        P(AXES, None),
        P(AXES, None),
        P(AXES, None),
        P(),
        P(),
        P(AXES, None, None, None),
        P(AXES, None, None),
        P(AXES, None, None),
    )
    out_specs = (P(AXES, None, None), P(AXES, None, None))
    return jax.shard_map(layer, mesh=mesh, in_specs=in_specs, out_specs=out_specs, check_vma=False)
```

```python
import functools

import jax
import jax.numpy as jnp
from jax import lax
from jax.experimental import pallas as pl
from jax.experimental.pallas import tpu as pltpu
from jax.sharding import PartitionSpec as P


SCALE = 2.0
SLOTS = 8
BASE = 4
EXTRA = 2
GROUP = 32
CHUNK = 512
AXES = ("dp", "expert")


def slot_table(experts, routing, probs, limit):
    tok_count = routing.shape[1]
    hit = [routing[k : k + 1, :] == experts for k in range(routing.shape[0])]
    member = sum(jnp.where(h, 1.0, 0.0) for h in hit)
    weight = sum(jnp.where(h, probs[k : k + 1, :], 0.0) for k, h in enumerate(hit))
    before = lax.broadcasted_iota(jnp.int32, (tok_count, tok_count), 0) < lax.broadcasted_iota(
        jnp.int32, (tok_count, tok_count), 1
    )
    rank = jnp.dot(
        member.astype(jnp.bfloat16),
        jnp.where(before, 1.0, 0.0).astype(jnp.bfloat16),
        preferred_element_type=jnp.float32,
    ).astype(jnp.int32)
    return jnp.where((member > 0.0) & (rank < limit), rank, -1), weight


def look_up(table, experts):
    lanes = lax.broadcasted_iota(jnp.int32, (experts.shape[0], table.shape[1]), 1)
    return jnp.sum(jnp.where(lanes == experts, table, 0), axis=1, keepdims=True)


def block_experts():
    first = pl.program_id(0) * GROUP
    return first + lax.broadcasted_iota(jnp.int32, (GROUP, 1), 0)


def spread(rank, weight, rows, count):
    group, tok_count = rank.shape
    parts = SLOTS // count
    sublane = lax.broadcasted_iota(jnp.int32, (group, SLOTS, tok_count), 1)
    match = rank[:, None, :] == sublane // parts
    factor = jnp.sum(jnp.where(match, weight[:, None, :], 0.0), axis=2, keepdims=True)
    width = rows.shape[1] // parts
    picks = [
        jnp.where(match & (sublane % parts == part), 1.0, 0.0).astype(jnp.bfloat16)
        for part in range(parts)
    ]
    stacked = [rows[:, part * width : (part + 1) * width] for part in range(parts)]
    picked = jnp.dot(
        jnp.concatenate(picks, axis=2).reshape(group * SLOTS, parts * tok_count),
        jnp.concatenate(stacked, axis=0),
        preferred_element_type=jnp.float32,
    )
    return (picked.reshape(group, SLOTS, width) * factor).astype(jnp.bfloat16)


def pack_kernel(
    half, room, routing, probs, marks, caps, own, tokens, cotangent, first, second
):
    tok_count, width = tokens.shape
    experts = block_experts()
    marked = look_up(marks[...], experts)
    limit = look_up(caps[...], experts) + room * marked
    rank, weight = slot_table(experts, routing[...], probs[...], limit)
    sublane = lax.broadcasted_iota(jnp.int32, (GROUP, SLOTS, tok_count), 1)
    pick = jnp.where(rank[:, None, :] == sublane, 1.0, 0.0).astype(jnp.bfloat16)
    rows = jnp.dot(
        pick.reshape(GROUP * SLOTS, tok_count), tokens[...], preferred_element_type=jnp.float32
    )
    first[:, :, :width] = rows.reshape(GROUP, SLOTS, width).astype(jnp.bfloat16)
    hot = jnp.where(marked == 1, experts, experts ^ half)
    hot_rank, hot_weight = slot_table(
        hot, routing[...], probs[...], look_up(caps[...], hot) + room
    )
    hot_rank = hot_rank - jnp.where(marked == 1, BASE, BASE + EXTRA)
    first[:, :, width:] = spread(hot_rank, hot_weight, cotangent, EXTRA)
    second[...] = spread(rank, weight, cotangent, BASE)


def pack(half, room, tables, arrays):
    experts = tables[2].shape[1]
    model_width = arrays[0].shape[1]
    operands = tables + arrays
    widths = (model_width + EXTRA * model_width // SLOTS, BASE * model_width // SLOTS)
    return pl.pallas_call(
        functools.partial(pack_kernel, half, room),
        grid=(experts // GROUP,),
        in_specs=[pl.BlockSpec(x.shape, lambda i: (0, 0)) for x in operands],
        out_specs=[pl.BlockSpec((GROUP, SLOTS, w), lambda i: (i, 0, 0)) for w in widths],
        out_shape=[jax.ShapeDtypeStruct((experts, SLOTS, w), jnp.bfloat16) for w in widths],
    )(*operands)


def choose(rows, columns, per_row, wanted):
    row = lax.broadcasted_iota(jnp.int32, (rows, columns), 0)
    column = lax.broadcasted_iota(jnp.int32, (rows, columns), 1)
    same = row // per_row == column // SLOTS
    hit = same & wanted(row % per_row, column % SLOTS)
    return jnp.where(hit, 1.0, 0.0).astype(jnp.bfloat16)


def prepare_kernel(low, hidden, wide_low, wide_hidden, own_low, own_hidden, far_low, far_hidden):
    block, rank_width = low.shape
    parts = SLOTS // BASE

    def take(matrix, array):
        return jnp.dot(matrix, array, preferred_element_type=jnp.float32)

    widen = choose(block, block, SLOTS, lambda i, m: i // parts == m)
    wide_hidden[...] = take(widen, hidden[...]).astype(jnp.bfloat16)
    rows_low = take(widen, jnp.tile(low[...], (1, parts)))
    part = lax.broadcasted_iota(jnp.int32, rows_low.shape, 0) % parts
    own = part == lax.broadcasted_iota(jnp.int32, rows_low.shape, 1) // rank_width
    wide_low[...] = jnp.where(own, rows_low, 0.0).astype(jnp.bfloat16)
    extra = own_low.shape[0]
    near = choose(extra, block, EXTRA, lambda i, m: i + BASE == m)
    own_low[...] = take(near, low[...]).astype(jnp.bfloat16)
    own_hidden[...] = take(near, hidden[...]).astype(jnp.bfloat16)
    far = choose(extra, block, EXTRA, lambda i, m: i + BASE + EXTRA == m)
    far_low[...] = take(far, low[...]).astype(jnp.bfloat16)
    far_hidden[...] = take(far, hidden[...]).astype(jnp.bfloat16)


def prepare(low, hidden):
    rows, rank_width = low.shape
    hidden_width = hidden.shape[1]
    block, extra = rows // 4, rows * EXTRA // SLOTS
    spec = lambda shape: pl.BlockSpec((shape[0] // 4, shape[1]), lambda i: (i, 0))
    shapes = [(rows, SLOTS // BASE * rank_width), (rows, hidden_width)]
    shapes += [(extra, rank_width), (extra, hidden_width)] * 2
    return pl.pallas_call(
        prepare_kernel,
        grid=(rows // block,),
        in_specs=[spec(low.shape), spec(hidden.shape)],
        out_specs=[spec(shape) for shape in shapes],
        out_shape=[jax.ShapeDtypeStruct(shape, jnp.bfloat16) for shape in shapes],
    )(low, hidden)


def finish_kernel(base, wide_low, wide_hidden, wide_out, grad_start, in_start, grad, in_grad, total):
    step = pl.program_id(0)
    block, width = base.shape
    parts, rank_width = SLOTS // BASE, grad.shape[0]
    for start in range(0, width, CHUNK):
        columns = slice(start, start + CHUNK)
        new = lax.dot_general(
            wide_low[...],
            base[:, columns],
            (((0,), (0,)), ((), ())),
            preferred_element_type=jnp.float32,
        )
        total[:, columns] = new + jnp.where(step == 0, 0.0, total[:, columns])
    halves = lax.dot_general(
        base[...], wide_out[...], (((1,), (1,)), ((), ())), preferred_element_type=jnp.float32
    )
    back = halves[:, :rank_width]
    for at in range(1, parts):
        later = halves[:, at * rank_width : (at + 1) * rank_width]
        back = back + pltpu.roll(later, block - at, 0)
    whole = lax.broadcasted_iota(jnp.int32, back.shape, 0) % parts == 0
    back = jnp.where(whole, SCALE * back, 0.0).astype(jnp.bfloat16)
    new_in = lax.dot_general(
        back, wide_hidden[...], (((0,), (0,)), ((), ())), preferred_element_type=jnp.float32
    )

    in_grad[...] = new_in + jnp.where(step == 0, in_start[...], in_grad[...])

    @pl.when(step == pl.num_programs(0) - 1)
    def _():
        for at in range(parts):
            columns = slice(at * width, (at + 1) * width)
            rows = slice(at * rank_width, (at + 1) * rank_width)
            grad[:, columns] = grad_start[:, columns] + total[rows, :]


def finish(base, wide_low, wide_hidden, wide_out, grad_start, in_start):
    rows, width = base.shape
    block = rows // 2
    row_block = lambda array: pl.BlockSpec((block, array.shape[1]), lambda i: (i, 0))
    kept = lambda array: pl.BlockSpec(array.shape, lambda i: (0, 0))
    return pl.pallas_call(
        finish_kernel,
        grid=(rows // block,),
        in_specs=[row_block(base), row_block(wide_low), row_block(wide_hidden)]
        + [kept(wide_out), kept(grad_start), kept(in_start)],
        out_specs=[kept(grad_start), kept(in_start)],
        out_shape=[
            jax.ShapeDtypeStruct(grad_start.shape, jnp.float32),
            jax.ShapeDtypeStruct(in_start.shape, jnp.float32),
        ],
        scratch_shapes=[pltpu.VMEM((wide_out.shape[0], width), jnp.float32)],
    )(base, wide_low, wide_hidden, wide_out, grad_start, in_start)


def exchange(block):
    return lax.all_to_all(block, AXES, split_axis=0, concat_axis=0, tiled=True)


def layer(
    tokens, cotangent, router_probs, routing, hot_marks, cap_counts, gate_up, adapter_in, adapter_out
):
    model_width = tokens.shape[1]
    experts = cap_counts.shape[0]
    n_expert = lax.axis_size("expert")
    half = n_expert // 2
    pairs = [(i, i ^ half) for i in range(n_expert)]
    own_index = lax.axis_index("dp") * n_expert + lax.axis_index("expert")
    own_marked = lax.dynamic_index_in_dim(hot_marks, own_index, 0, keepdims=False) == 1
    own_in, own_out = adapter_in[0], adapter_out[0]

    partner_out = lax.ppermute(own_out, "expert", pairs)
    room = tokens.shape[0] * routing.shape[1] // experts
    tables = (
        routing.T,
        router_probs.T,
        hot_marks[None, :],
        cap_counts[None, :],
        own_marked.astype(jnp.int32).reshape(1, 1),
    )
    first, second = pack(half, room, tables, (tokens, cotangent))
    first = exchange(first)
    second = exchange(second)

    inputs = first[:, :, :model_width].reshape(experts * SLOTS, model_width)
    gate_out = jnp.dot(inputs, gate_up[0, 0], preferred_element_type=jnp.float32)
    up_out = jnp.dot(inputs, gate_up[0, 1], preferred_element_type=jnp.float32)
    hidden = (jax.nn.silu(gate_out) * up_out).astype(jnp.bfloat16)
    low = (
        SCALE * jnp.einsum("nf,rf->nr", hidden, own_in, preferred_element_type=jnp.float32)
    ).astype(jnp.bfloat16)
    wide_low, wide_hidden, own_low, own_hidden, far_low, far_hidden = prepare(low, hidden)

    parts = SLOTS // EXTRA
    extra = first[:, :, model_width:].reshape(experts, EXTRA, parts, model_width // parts)
    extra = extra.reshape(experts * EXTRA, model_width)
    work_out = jnp.where(own_marked, own_out, partner_out)
    extra_back = (
        SCALE * jnp.einsum("nd,rd->nr", extra, work_out, preferred_element_type=jnp.float32)
    ).astype(jnp.bfloat16)
    swapped = lax.ppermute(jnp.where(own_marked, far_low, extra_back), "expert", pairs)
    extra_low = jnp.where(own_marked, own_low, swapped)
    extra_grad = jnp.einsum("nr,nd->rd", extra_low, extra, preferred_element_type=jnp.float32)
    returned = lax.ppermute(extra_grad, "expert", pairs)
    in_start = jnp.einsum("nr,nf->rf", extra_back, own_hidden, preferred_element_type=jnp.float32)
    in_start += jnp.einsum("nr,nf->rf", swapped, far_hidden, preferred_element_type=jnp.float32)

    parts, width = SLOTS // BASE, BASE * model_width // SLOTS
    wide_out = jnp.concatenate(
        [own_out[:, at * width : (at + 1) * width] for at in range(parts)], axis=0
    )
    grad, in_grad = finish(
        second.reshape(experts * SLOTS, width),
        wide_low,
        wide_hidden,
        wide_out,
        jnp.where(own_marked, extra_grad, 0.0),
        jnp.where(own_marked, in_start, 0.0),
    )
    out_grad = grad + jnp.where(own_marked, returned, 0.0)
    return in_grad[None], out_grad[None]


def solution(mesh):
    in_specs = (
        P(AXES, None),
        P(AXES, None),
        P(AXES, None),
        P(AXES, None),
        P(),
        P(),
        P(AXES, None, None, None),
        P(AXES, None, None),
        P(AXES, None, None),
    )
    out_specs = (P(AXES, None, None), P(AXES, None, None))
    return jax.shard_map(layer, mesh=mesh, in_specs=in_specs, out_specs=out_specs, check_vma=False)
```

```python
import functools

import jax
import jax.numpy as jnp
from jax import lax
from jax.experimental import pallas as pl
from jax.experimental.pallas import tpu as pltpu
from jax.sharding import PartitionSpec as P


SCALE = 2.0
SLOTS = 8
BASE = 4
EXTRA = 2
GROUP = 32
CHUNK = 512
AXES = ("dp", "expert")


def slot_table(experts, routing, probs, limit):
    tok_count = routing.shape[1]
    hit = [routing[k : k + 1, :] == experts for k in range(routing.shape[0])]
    member = sum(jnp.where(h, 1.0, 0.0) for h in hit)
    weight = sum(jnp.where(h, probs[k : k + 1, :], 0.0) for k, h in enumerate(hit))
    before = lax.broadcasted_iota(jnp.int32, (tok_count, tok_count), 0) < lax.broadcasted_iota(
        jnp.int32, (tok_count, tok_count), 1
    )
    rank = jnp.dot(
        member.astype(jnp.bfloat16),
        jnp.where(before, 1.0, 0.0).astype(jnp.bfloat16),
        preferred_element_type=jnp.float32,
    ).astype(jnp.int32)
    return jnp.where((member > 0.0) & (rank < limit), rank, -1), weight


def look_up(table, experts):
    lanes = lax.broadcasted_iota(jnp.int32, (experts.shape[0], table.shape[1]), 1)
    return jnp.sum(jnp.where(lanes == experts, table, 0), axis=1, keepdims=True)


def block_experts():
    first = pl.program_id(0) * GROUP
    return first + lax.broadcasted_iota(jnp.int32, (GROUP, 1), 0)


def spread(rank, weight, rows, count):
    group, tok_count = rank.shape
    parts = SLOTS // count
    sublane = lax.broadcasted_iota(jnp.int32, (group, SLOTS, tok_count), 1)
    match = rank[:, None, :] == sublane // parts
    factor = jnp.sum(jnp.where(match, weight[:, None, :], 0.0), axis=2, keepdims=True)
    width = rows.shape[1] // parts
    picks = [
        jnp.where(match & (sublane % parts == part), 1.0, 0.0).astype(jnp.bfloat16)
        for part in range(parts)
    ]
    stacked = [rows[:, part * width : (part + 1) * width] for part in range(parts)]
    picked = jnp.dot(
        jnp.concatenate(picks, axis=2).reshape(group * SLOTS, parts * tok_count),
        jnp.concatenate(stacked, axis=0),
        preferred_element_type=jnp.float32,
    )
    return (picked.reshape(group, SLOTS, width) * factor).astype(jnp.bfloat16)


def pack_kernel(
    half, room, routing, probs, marks, caps, own, tokens, cotangent, first, second
):
    tok_count, width = tokens.shape
    experts = block_experts()
    marked = look_up(marks[...], experts)
    limit = look_up(caps[...], experts) + room * marked
    rank, weight = slot_table(experts, routing[...], probs[...], limit)
    sublane = lax.broadcasted_iota(jnp.int32, (GROUP, SLOTS, tok_count), 1)
    pick = jnp.where(rank[:, None, :] == sublane, 1.0, 0.0).astype(jnp.bfloat16)
    rows = jnp.dot(
        pick.reshape(GROUP * SLOTS, tok_count), tokens[...], preferred_element_type=jnp.float32
    )
    first[:, :, :width] = rows.reshape(GROUP, SLOTS, width).astype(jnp.bfloat16)
    hot = jnp.where(marked == 1, experts, experts ^ half)
    hot_rank, hot_weight = slot_table(
        hot, routing[...], probs[...], look_up(caps[...], hot) + room
    )
    hot_rank = hot_rank - jnp.where(marked == 1, BASE, BASE + EXTRA)
    first[:, :, width:] = spread(hot_rank, hot_weight, cotangent, EXTRA)
    second[...] = spread(rank, weight, cotangent, BASE)


def pack(half, room, tables, arrays):
    experts = tables[2].shape[1]
    model_width = arrays[0].shape[1]
    operands = tables + arrays
    widths = (model_width + EXTRA * model_width // SLOTS, BASE * model_width // SLOTS)
    return pl.pallas_call(
        functools.partial(pack_kernel, half, room),
        grid=(experts // GROUP,),
        in_specs=[pl.BlockSpec(x.shape, lambda i: (0, 0)) for x in operands],
        out_specs=[pl.BlockSpec((GROUP, SLOTS, w), lambda i: (i, 0, 0)) for w in widths],
        out_shape=[jax.ShapeDtypeStruct((experts, SLOTS, w), jnp.bfloat16) for w in widths],
    )(*operands)


def choose(rows, columns, per_row, wanted):
    row = lax.broadcasted_iota(jnp.int32, (rows, columns), 0)
    column = lax.broadcasted_iota(jnp.int32, (rows, columns), 1)
    same = row // per_row == column // SLOTS
    hit = same & wanted(row % per_row, column % SLOTS)
    return jnp.where(hit, 1.0, 0.0).astype(jnp.bfloat16)


def prepare_kernel(low, hidden, wide_low, wide_hidden, own_low, own_hidden, far_low, far_hidden):
    block, rank_width = low.shape
    parts = SLOTS // BASE

    def take(matrix, array):
        return jnp.dot(matrix, array, preferred_element_type=jnp.float32)

    widen = choose(block, block, SLOTS, lambda i, m: i // parts == m)
    wide_hidden[...] = take(widen, hidden[...]).astype(jnp.bfloat16)
    rows_low = take(widen, jnp.tile(low[...], (1, parts)))
    part = lax.broadcasted_iota(jnp.int32, rows_low.shape, 0) % parts
    own = part == lax.broadcasted_iota(jnp.int32, rows_low.shape, 1) // rank_width
    wide_low[...] = jnp.where(own, rows_low, 0.0).astype(jnp.bfloat16)
    extra = own_low.shape[0]
    near = choose(extra, block, EXTRA, lambda i, m: i + BASE == m)
    own_low[...] = take(near, low[...]).astype(jnp.bfloat16)
    own_hidden[...] = take(near, hidden[...]).astype(jnp.bfloat16)
    far = choose(extra, block, EXTRA, lambda i, m: i + BASE + EXTRA == m)
    far_low[...] = take(far, low[...]).astype(jnp.bfloat16)
    far_hidden[...] = take(far, hidden[...]).astype(jnp.bfloat16)


def prepare(low, hidden):
    rows, rank_width = low.shape
    hidden_width = hidden.shape[1]
    block, extra = rows // 4, rows * EXTRA // SLOTS
    spec = lambda shape: pl.BlockSpec((shape[0] // 4, shape[1]), lambda i: (i, 0))
    shapes = [(rows, SLOTS // BASE * rank_width), (rows, hidden_width)]
    shapes += [(extra, rank_width), (extra, hidden_width)] * 2
    return pl.pallas_call(
        prepare_kernel,
        grid=(rows // block,),
        in_specs=[spec(low.shape), spec(hidden.shape)],
        out_specs=[spec(shape) for shape in shapes],
        out_shape=[jax.ShapeDtypeStruct(shape, jnp.bfloat16) for shape in shapes],
    )(low, hidden)


def finish_kernel(base, wide_low, wide_hidden, own_out, grad_start, grad, in_grad, total):
    step = pl.program_id(0)
    block, width = base.shape
    parts, rank_width = SLOTS // BASE, grad.shape[0]
    for start in range(0, width, CHUNK):
        columns = slice(start, start + CHUNK)
        new = lax.dot_general(
            wide_low[...],
            base[:, columns],
            (((0,), (0,)), ((), ())),
            preferred_element_type=jnp.float32,
        )
        total[:, columns] = new + jnp.where(step == 0, 0.0, total[:, columns])
    wide_out = [own_out[:, at * width : (at + 1) * width] for at in range(parts)]
    halves = lax.dot_general(
        base[...],
        jnp.concatenate(wide_out, axis=0),
        (((1,), (1,)), ((), ())),
        preferred_element_type=jnp.float32,
    )
    back = halves[:, :rank_width]
    for at in range(1, parts):
        later = halves[:, at * rank_width : (at + 1) * rank_width]
        back = back + pltpu.roll(later, block - at, 0)
    whole = lax.broadcasted_iota(jnp.int32, back.shape, 0) % parts == 0
    back = jnp.where(whole, SCALE * back, 0.0).astype(jnp.bfloat16)
    new_in = lax.dot_general(
        back, wide_hidden[...], (((0,), (0,)), ((), ())), preferred_element_type=jnp.float32
    )

    in_grad[...] = new_in + jnp.where(step == 0, 0.0, in_grad[...])

    @pl.when(step == pl.num_programs(0) - 1)
    def _():
        for at in range(parts):
            columns = slice(at * width, (at + 1) * width)
            rows = slice(at * rank_width, (at + 1) * rank_width)
            grad[:, columns] = grad_start[:, columns] + total[rows, :]


def finish(base, wide_low, wide_hidden, own_out, grad_start):
    rows, width = base.shape
    block = rows // 2
    rank_width, hidden_width = own_out.shape[0], wide_hidden.shape[1]
    row_block = lambda array: pl.BlockSpec((block, array.shape[1]), lambda i: (i, 0))
    kept = lambda shape: pl.BlockSpec(shape, lambda i: (0, 0))
    out_shapes = (grad_start.shape, (rank_width, hidden_width))
    return pl.pallas_call(
        finish_kernel,
        grid=(rows // block,),
        in_specs=[row_block(base), row_block(wide_low), row_block(wide_hidden)]
        + [kept(own_out.shape), kept(grad_start.shape)],
        out_specs=[kept(shape) for shape in out_shapes],
        out_shape=[jax.ShapeDtypeStruct(shape, jnp.float32) for shape in out_shapes],
        scratch_shapes=[pltpu.VMEM((wide_low.shape[1], width), jnp.float32)],
    )(base, wide_low, wide_hidden, own_out, grad_start)


def exchange(block):
    return lax.all_to_all(block, AXES, split_axis=0, concat_axis=0, tiled=True)


def layer(
    tokens, cotangent, router_probs, routing, hot_marks, cap_counts, gate_up, adapter_in, adapter_out
):
    model_width = tokens.shape[1]
    experts = cap_counts.shape[0]
    n_expert = lax.axis_size("expert")
    half = n_expert // 2
    pairs = [(i, i ^ half) for i in range(n_expert)]
    own_index = lax.axis_index("dp") * n_expert + lax.axis_index("expert")
    own_in, own_out = adapter_in[0], adapter_out[0]

    partner_out = lax.ppermute(own_out, "expert", pairs)
    room = tokens.shape[0] * routing.shape[1] // experts
    tables = (
        routing.T,
        router_probs.T,
        hot_marks[None, :],
        cap_counts[None, :],
        own_index.reshape(1, 1),
    )
    first, second = pack(half, room, tables, (tokens, cotangent))
    first = exchange(first)
    own_index += jnp.isnan(first[0, 0, 0]).astype(jnp.int32)
    own_marked = lax.dynamic_index_in_dim(hot_marks, own_index, 0, keepdims=False) == 1
    second = exchange(second)

    inputs = first[:, :, :model_width].reshape(experts * SLOTS, model_width)
    gate_out = jnp.dot(inputs, gate_up[0, 0], preferred_element_type=jnp.float32)
    up_out = jnp.dot(inputs, gate_up[0, 1], preferred_element_type=jnp.float32)
    hidden = (jax.nn.silu(gate_out) * up_out).astype(jnp.bfloat16)
    low = (
        SCALE * jnp.einsum("nf,rf->nr", hidden, own_in, preferred_element_type=jnp.float32)
    ).astype(jnp.bfloat16)
    wide_low, wide_hidden, own_low, own_hidden, far_low, far_hidden = prepare(low, hidden)

    parts = SLOTS // EXTRA
    extra = first[:, :, model_width:].reshape(experts, EXTRA, parts, model_width // parts)
    extra = extra.reshape(experts * EXTRA, model_width)
    work_out = jnp.where(own_marked, own_out, partner_out)
    extra_back = (
        SCALE * jnp.einsum("nd,rd->nr", extra, work_out, preferred_element_type=jnp.float32)
    ).astype(jnp.bfloat16)
    swapped = lax.ppermute(jnp.where(own_marked, far_low, extra_back), "expert", pairs)
    extra_low = jnp.where(own_marked, own_low, swapped)
    extra_grad = jnp.einsum("nr,nd->rd", extra_low, extra, preferred_element_type=jnp.float32)
    returned = lax.ppermute(extra_grad.astype(jnp.bfloat16), "expert", pairs)
    in_start = jnp.einsum("nr,nf->rf", extra_back, own_hidden, preferred_element_type=jnp.float32)
    in_start += jnp.einsum("nr,nf->rf", swapped, far_hidden, preferred_element_type=jnp.float32)
    grad, in_grad = finish(
        second.reshape(experts * SLOTS, BASE * model_width // SLOTS),
        wide_low,
        wide_hidden,
        own_out,
        jnp.where(own_marked, extra_grad, 0.0),
    )
    in_grad = in_grad + jnp.where(own_marked, in_start, 0.0)
    out_grad = grad + jnp.where(own_marked, returned.astype(jnp.float32), 0.0)
    return in_grad[None], out_grad[None]


def solution(mesh):
    in_specs = (
        P(AXES, None),
        P(AXES, None),
        P(AXES, None),
        P(AXES, None),
        P(),
        P(),
        P(AXES, None, None, None),
        P(AXES, None, None),
        P(AXES, None, None),
    )
    out_specs = (P(AXES, None, None), P(AXES, None, None))
    return jax.shard_map(layer, mesh=mesh, in_specs=in_specs, out_specs=out_specs, check_vma=False)
```

```python
import functools

import jax
import jax.numpy as jnp
from jax import lax
from jax.experimental import pallas as pl
from jax.experimental.pallas import tpu as pltpu
from jax.sharding import PartitionSpec as P


SCALE = 2.0
SLOTS = 8
BASE = 4
EXTRA = 2
GROUP = 32
CHUNK = 512
AXES = ("dp", "expert")


def slot_table(experts, routing, probs, limit):
    tok_count = routing.shape[1]
    hit = [routing[k : k + 1, :] == experts for k in range(routing.shape[0])]
    member = sum(jnp.where(h, 1.0, 0.0) for h in hit)
    weight = sum(jnp.where(h, probs[k : k + 1, :], 0.0) for k, h in enumerate(hit))
    before = lax.broadcasted_iota(jnp.int32, (tok_count, tok_count), 0) < lax.broadcasted_iota(
        jnp.int32, (tok_count, tok_count), 1
    )
    rank = jnp.dot(
        member.astype(jnp.bfloat16),
        jnp.where(before, 1.0, 0.0).astype(jnp.bfloat16),
        preferred_element_type=jnp.float32,
    ).astype(jnp.int32)
    return jnp.where((member > 0.0) & (rank < limit), rank, -1), weight


def look_up(table, experts):
    lanes = lax.broadcasted_iota(jnp.int32, (experts.shape[0], table.shape[1]), 1)
    return jnp.sum(jnp.where(lanes == experts, table, 0), axis=1, keepdims=True)


def block_experts():
    first = pl.program_id(0) * GROUP
    return first + lax.broadcasted_iota(jnp.int32, (GROUP, 1), 0)


def spread(rank, weight, rows, count):
    group, tok_count = rank.shape
    parts = SLOTS // count
    sublane = lax.broadcasted_iota(jnp.int32, (group, SLOTS, tok_count), 1)
    match = rank[:, None, :] == sublane // parts
    factor = jnp.sum(jnp.where(match, weight[:, None, :], 0.0), axis=2, keepdims=True)
    width = rows.shape[1] // parts
    picks = [
        jnp.where(match & (sublane % parts == part), 1.0, 0.0).astype(jnp.bfloat16)
        for part in range(parts)
    ]
    stacked = [rows[:, part * width : (part + 1) * width] for part in range(parts)]
    picked = jnp.dot(
        jnp.concatenate(picks, axis=2).reshape(group * SLOTS, parts * tok_count),
        jnp.concatenate(stacked, axis=0),
        preferred_element_type=jnp.float32,
    )
    return (picked.reshape(group, SLOTS, width) * factor).astype(jnp.bfloat16)


def pack_kernel(
    half, room, routing, probs, marks, caps, own, tokens, cotangent, first, second
):
    tok_count, width = tokens.shape
    experts = block_experts()
    marked = look_up(marks[...], experts)
    limit = look_up(caps[...], experts) + room * marked
    rank, weight = slot_table(experts, routing[...], probs[...], limit)
    sublane = lax.broadcasted_iota(jnp.int32, (GROUP, SLOTS, tok_count), 1)
    pick = jnp.where(rank[:, None, :] == sublane, 1.0, 0.0).astype(jnp.bfloat16)
    rows = jnp.dot(
        pick.reshape(GROUP * SLOTS, tok_count), tokens[...], preferred_element_type=jnp.float32
    )
    first[:, :, :width] = rows.reshape(GROUP, SLOTS, width).astype(jnp.bfloat16)
    hot = jnp.where(marked == 1, experts, experts ^ half)
    hot_rank, hot_weight = slot_table(
        hot, routing[...], probs[...], look_up(caps[...], hot) + room
    )
    hot_rank = hot_rank - jnp.where(marked == 1, BASE, BASE + EXTRA)
    first[:, :, width:] = spread(hot_rank, hot_weight, cotangent, EXTRA)
    second[...] = spread(rank, weight, cotangent, BASE)


def pack(half, room, tables, arrays):
    experts = tables[2].shape[1]
    model_width = arrays[0].shape[1]
    operands = tables + arrays
    widths = (model_width + EXTRA * model_width // SLOTS, BASE * model_width // SLOTS)
    return pl.pallas_call(
        functools.partial(pack_kernel, half, room),
        grid=(experts // GROUP,),
        in_specs=[pl.BlockSpec(x.shape, lambda i: (0, 0)) for x in operands],
        out_specs=[pl.BlockSpec((GROUP, SLOTS, w), lambda i: (i, 0, 0)) for w in widths],
        out_shape=[jax.ShapeDtypeStruct((experts, SLOTS, w), jnp.bfloat16) for w in widths],
    )(*operands)


def choose(rows, columns, per_row, wanted):
    row = lax.broadcasted_iota(jnp.int32, (rows, columns), 0)
    column = lax.broadcasted_iota(jnp.int32, (rows, columns), 1)
    same = row // per_row == column // SLOTS
    hit = same & wanted(row % per_row, column % SLOTS)
    return jnp.where(hit, 1.0, 0.0).astype(jnp.bfloat16)


def prepare_kernel(low, hidden, wide_low, wide_hidden, own_low, own_hidden, far_low, far_hidden):
    block, rank_width = low.shape
    parts = SLOTS // BASE

    def take(matrix, array):
        return jnp.dot(matrix, array, preferred_element_type=jnp.float32)

    widen = choose(block, block, SLOTS, lambda i, m: i // parts == m)
    wide_hidden[...] = take(widen, hidden[...]).astype(jnp.bfloat16)
    rows_low = take(widen, jnp.tile(low[...], (1, parts)))
    part = lax.broadcasted_iota(jnp.int32, rows_low.shape, 0) % parts
    own = part == lax.broadcasted_iota(jnp.int32, rows_low.shape, 1) // rank_width
    wide_low[...] = jnp.where(own, rows_low, 0.0).astype(jnp.bfloat16)
    extra = own_low.shape[0]
    near = choose(extra, block, EXTRA, lambda i, m: i + BASE == m)
    own_low[...] = take(near, low[...]).astype(jnp.bfloat16)
    own_hidden[...] = take(near, hidden[...]).astype(jnp.bfloat16)
    far = choose(extra, block, EXTRA, lambda i, m: i + BASE + EXTRA == m)
    far_low[...] = take(far, low[...]).astype(jnp.bfloat16)
    far_hidden[...] = take(far, hidden[...]).astype(jnp.bfloat16)


def prepare(low, hidden):
    rows, rank_width = low.shape
    hidden_width = hidden.shape[1]
    block, extra = rows // 4, rows * EXTRA // SLOTS
    spec = lambda shape: pl.BlockSpec((shape[0] // 4, shape[1]), lambda i: (i, 0))
    shapes = [(rows, SLOTS // BASE * rank_width), (rows, hidden_width)]
    shapes += [(extra, rank_width), (extra, hidden_width)] * 2
    return pl.pallas_call(
        prepare_kernel,
        grid=(rows // block,),
        in_specs=[spec(low.shape), spec(hidden.shape)],
        out_specs=[spec(shape) for shape in shapes],
        out_shape=[jax.ShapeDtypeStruct(shape, jnp.bfloat16) for shape in shapes],
    )(low, hidden)


def finish_kernel(
    base,
    wide_low,
    wide_hidden,
    own_out,
    near_back,
    near_hidden,
    far_back,
    far_hidden,
    grad,
    in_grad,
    total,
):
    step = pl.program_id(0)
    block, width = base.shape
    parts, rank_width = SLOTS // BASE, grad.shape[0]
    for start in range(0, width, CHUNK):
        columns = slice(start, start + CHUNK)
        new = lax.dot_general(
            wide_low[...],
            base[:, columns],
            (((0,), (0,)), ((), ())),
            preferred_element_type=jnp.float32,
        )
        total[:, columns] = new + jnp.where(step == 0, 0.0, total[:, columns])
    wide_out = [own_out[:, at * width : (at + 1) * width] for at in range(parts)]
    halves = lax.dot_general(
        base[...],
        jnp.concatenate(wide_out, axis=0),
        (((1,), (1,)), ((), ())),
        preferred_element_type=jnp.float32,
    )
    back = halves[:, :rank_width]
    for at in range(1, parts):
        later = halves[:, at * rank_width : (at + 1) * rank_width]
        back = back + pltpu.roll(later, block - at, 0)
    whole = lax.broadcasted_iota(jnp.int32, back.shape, 0) % parts == 0
    back = jnp.where(whole, SCALE * back, 0.0).astype(jnp.bfloat16)
    new_in = lax.dot_general(
        back, wide_hidden[...], (((0,), (0,)), ((), ())), preferred_element_type=jnp.float32
    )


    @pl.when(step == 0)
    def _():
        start = new_in
        for back_rows, hidden_rows in ((near_back, near_hidden), (far_back, far_hidden)):
            start = start + lax.dot_general(
                back_rows[...],
                hidden_rows[...],
                (((0,), (0,)), ((), ())),
                preferred_element_type=jnp.float32,
            )
        in_grad[...] = start

    @pl.when(step > 0)
    def _():
        in_grad[...] += new_in

    @pl.when(step == pl.num_programs(0) - 1)
    def _():
        for at in range(parts):
            columns = slice(at * width, (at + 1) * width)
            rows = slice(at * rank_width, (at + 1) * rank_width)
            grad[:, columns] = total[rows, :]


def finish(base, wide_low, wide_hidden, *whole):
    rows, width = base.shape
    block = rows // 2
    own_out = whole[0]
    row_block = lambda array: pl.BlockSpec((block, array.shape[1]), lambda i: (i, 0))
    kept = lambda shape: pl.BlockSpec(shape, lambda i: (0, 0))
    out_shapes = (own_out.shape, (own_out.shape[0], wide_hidden.shape[1]))
    return pl.pallas_call(
        finish_kernel,
        grid=(rows // block,),
        in_specs=[row_block(x) for x in (base, wide_low, wide_hidden)]
        + [kept(x.shape) for x in whole],
        out_specs=[kept(shape) for shape in out_shapes],
        out_shape=[jax.ShapeDtypeStruct(shape, jnp.float32) for shape in out_shapes],
        scratch_shapes=[pltpu.VMEM((wide_low.shape[1], width), jnp.float32)],
    )(base, wide_low, wide_hidden, *whole)


def exchange(block):
    return lax.all_to_all(block, AXES, split_axis=0, concat_axis=0, tiled=True)


def layer(
    tokens, cotangent, router_probs, routing, hot_marks, cap_counts, gate_up, adapter_in, adapter_out
):
    model_width = tokens.shape[1]
    experts = cap_counts.shape[0]
    n_expert = lax.axis_size("expert")
    half = n_expert // 2
    pairs = [(i, i ^ half) for i in range(n_expert)]
    own_index = lax.axis_index("dp") * n_expert + lax.axis_index("expert")
    own_in, own_out = adapter_in[0], adapter_out[0]

    partner_out = lax.ppermute(own_out, "expert", pairs)
    room = tokens.shape[0] * routing.shape[1] // experts
    tables = (
        routing.T,
        router_probs.T,
        hot_marks[None, :],
        cap_counts[None, :],
        own_index.reshape(1, 1),
    )
    first, second = pack(half, room, tables, (tokens, cotangent))
    first = exchange(first)
    own_index += jnp.isnan(first[0, 0, 0]).astype(jnp.int32)
    own_marked = lax.dynamic_index_in_dim(hot_marks, own_index, 0, keepdims=False) == 1
    second = exchange(second)

    inputs = first[:, :, :model_width].reshape(experts * SLOTS, model_width)
    gate_out = jnp.dot(inputs, gate_up[0, 0], preferred_element_type=jnp.float32)
    up_out = jnp.dot(inputs, gate_up[0, 1], preferred_element_type=jnp.float32)
    hidden = (jax.nn.silu(gate_out) * up_out).astype(jnp.bfloat16)
    low = (
        SCALE * jnp.einsum("nf,rf->nr", hidden, own_in, preferred_element_type=jnp.float32)
    ).astype(jnp.bfloat16)
    wide_low, wide_hidden, own_low, own_hidden, far_low, far_hidden = prepare(low, hidden)

    parts = SLOTS // EXTRA
    extra = first[:, :, model_width:].reshape(experts, EXTRA, parts, model_width // parts)
    extra = extra.reshape(experts * EXTRA, model_width)
    work_out = jnp.where(own_marked, own_out, partner_out)
    extra_back = (
        SCALE * jnp.einsum("nd,rd->nr", extra, work_out, preferred_element_type=jnp.float32)
    ).astype(jnp.bfloat16)
    swapped = lax.ppermute(jnp.where(own_marked, far_low, extra_back), "expert", pairs)
    extra_low = jnp.where(own_marked, own_low, swapped)
    extra_grad = jnp.einsum("nr,nd->rd", extra_low, extra, preferred_element_type=jnp.float32)
    returned = lax.ppermute(extra_grad.astype(jnp.bfloat16), "expert", pairs)
    grad, in_grad = finish(
        second.reshape(experts * SLOTS, BASE * model_width // SLOTS),
        wide_low,
        wide_hidden,
        own_out,
        extra_back,
        own_hidden,
        swapped,
        far_hidden,
    )
    out_grad = grad + jnp.where(own_marked, extra_grad + returned.astype(jnp.float32), 0.0)
    return in_grad[None], out_grad[None]


def solution(mesh):
    in_specs = (
        P(AXES, None),
        P(AXES, None),
        P(AXES, None),
        P(AXES, None),
        P(),
        P(),
        P(AXES, None, None, None),
        P(AXES, None, None),
        P(AXES, None, None),
    )
    out_specs = (P(AXES, None, None), P(AXES, None, None))
    return jax.shard_map(layer, mesh=mesh, in_specs=in_specs, out_specs=out_specs, check_vma=False)
```

```python
import functools

import jax
import jax.numpy as jnp
from jax import lax
from jax.experimental import pallas as pl
from jax.experimental.pallas import tpu as pltpu
from jax.sharding import PartitionSpec as P


SCALE = 2.0
SLOTS = 8
BASE = 4
EXTRA = 2
GROUP = 64
CHUNK = 512
AXES = ("dp", "expert")


def slot_table(experts, routing, probs, limit):
    tok_count = routing.shape[1]
    hit = [routing[k : k + 1, :] == experts for k in range(routing.shape[0])]
    member = sum(jnp.where(h, 1.0, 0.0) for h in hit)
    weight = sum(jnp.where(h, probs[k : k + 1, :], 0.0) for k, h in enumerate(hit))
    before = lax.broadcasted_iota(jnp.int32, (tok_count, tok_count), 0) < lax.broadcasted_iota(
        jnp.int32, (tok_count, tok_count), 1
    )
    rank = jnp.dot(
        member.astype(jnp.bfloat16),
        jnp.where(before, 1.0, 0.0).astype(jnp.bfloat16),
        preferred_element_type=jnp.float32,
    ).astype(jnp.int32)
    return jnp.where((member > 0.0) & (rank < limit), rank, -1), weight


def look_up(table, experts):
    lanes = lax.broadcasted_iota(jnp.int32, (experts.shape[0], table.shape[1]), 1)
    return jnp.sum(jnp.where(lanes == experts, table, 0), axis=1, keepdims=True)


def block_experts():
    first = pl.program_id(0) * GROUP
    return first + lax.broadcasted_iota(jnp.int32, (GROUP, 1), 0)


def spread(rank, weight, rows, count):
    group, tok_count = rank.shape
    parts = SLOTS // count
    sublane = lax.broadcasted_iota(jnp.int32, (group, SLOTS, tok_count), 1)
    match = rank[:, None, :] == sublane // parts
    factor = jnp.sum(jnp.where(match, weight[:, None, :], 0.0), axis=2, keepdims=True)
    width = rows.shape[1] // parts
    picks = [
        jnp.where(match & (sublane % parts == part), 1.0, 0.0).astype(jnp.bfloat16)
        for part in range(parts)
    ]
    stacked = [rows[:, part * width : (part + 1) * width] for part in range(parts)]
    picked = jnp.dot(
        jnp.concatenate(picks, axis=2).reshape(group * SLOTS, parts * tok_count),
        jnp.concatenate(stacked, axis=0),
        preferred_element_type=jnp.float32,
    )
    return (picked.reshape(group, SLOTS, width) * factor).astype(jnp.bfloat16)


def pack_kernel(
    half, room, routing, probs, marks, caps, own, tokens, cotangent, first, second
):
    tok_count, width = tokens.shape
    experts = block_experts()
    marked = look_up(marks[...], experts)
    limit = look_up(caps[...], experts) + room * marked
    rank, weight = slot_table(experts, routing[...], probs[...], limit)
    sublane = lax.broadcasted_iota(jnp.int32, (GROUP, SLOTS, tok_count), 1)
    pick = jnp.where(rank[:, None, :] == sublane, 1.0, 0.0).astype(jnp.bfloat16)
    rows = jnp.dot(
        pick.reshape(GROUP * SLOTS, tok_count), tokens[...], preferred_element_type=jnp.float32
    )
    here = pl.ds(pl.program_id(0) * GROUP, GROUP)
    first[here, :, :width] = rows.reshape(GROUP, SLOTS, width).astype(jnp.bfloat16)
    hot = jnp.where(marked == 1, experts, experts ^ half)
    hot_rank, hot_weight = slot_table(
        hot, routing[...], probs[...], look_up(caps[...], hot) + room
    )
    hot_rank = hot_rank - jnp.where(marked == 1, BASE, BASE + EXTRA)
    first[here, :, width:] = spread(hot_rank, hot_weight, cotangent, EXTRA)
    second[here, :, :] = spread(rank, weight, cotangent, BASE)


def pack(half, room, tables, arrays):
    experts = tables[2].shape[1]
    model_width = arrays[0].shape[1]
    operands = tables + arrays
    widths = (model_width + EXTRA * model_width // SLOTS, BASE * model_width // SLOTS)
    return pl.pallas_call(
        functools.partial(pack_kernel, half, room),
        grid=(experts // GROUP,),
        in_specs=[pl.BlockSpec(x.shape, lambda i: (0, 0)) for x in operands],
        out_specs=[pl.BlockSpec(memory_space=pltpu.VMEM) for w in widths],
        out_shape=[pltpu.VMEM((experts, SLOTS, w), jnp.bfloat16) for w in widths],
        compiler_params=pltpu.CompilerParams(vmem_limit_bytes=50200 << 10),
    )(*operands)


def choose(rows, columns, per_row, wanted):
    row = lax.broadcasted_iota(jnp.int32, (rows, columns), 0)
    column = lax.broadcasted_iota(jnp.int32, (rows, columns), 1)
    same = row // per_row == column // SLOTS
    hit = same & wanted(row % per_row, column % SLOTS)
    return jnp.where(hit, 1.0, 0.0).astype(jnp.bfloat16)


def prepare_kernel(low, hidden, wide_low, wide_hidden, own_low, own_hidden, far_low, far_hidden):
    block, rank_width = low.shape
    parts = SLOTS // BASE

    def take(matrix, array):
        return jnp.dot(matrix, array, preferred_element_type=jnp.float32)

    widen = choose(block, block, SLOTS, lambda i, m: i // parts == m)
    wide_hidden[...] = take(widen, hidden[...]).astype(jnp.bfloat16)
    rows_low = take(widen, jnp.tile(low[...], (1, parts)))
    part = lax.broadcasted_iota(jnp.int32, rows_low.shape, 0) % parts
    own = part == lax.broadcasted_iota(jnp.int32, rows_low.shape, 1) // rank_width
    wide_low[...] = jnp.where(own, rows_low, 0.0).astype(jnp.bfloat16)
    extra = own_low.shape[0]
    near = choose(extra, block, EXTRA, lambda i, m: i + BASE == m)
    own_low[...] = take(near, low[...]).astype(jnp.bfloat16)
    own_hidden[...] = take(near, hidden[...]).astype(jnp.bfloat16)
    far = choose(extra, block, EXTRA, lambda i, m: i + BASE + EXTRA == m)
    far_low[...] = take(far, low[...]).astype(jnp.bfloat16)
    far_hidden[...] = take(far, hidden[...]).astype(jnp.bfloat16)


def prepare(low, hidden):
    rows, rank_width = low.shape
    hidden_width = hidden.shape[1]
    block, extra = rows // 4, rows * EXTRA // SLOTS
    spec = lambda shape: pl.BlockSpec((shape[0] // 4, shape[1]), lambda i: (i, 0))
    shapes = [(rows, SLOTS // BASE * rank_width), (rows, hidden_width)]
    shapes += [(extra, rank_width), (extra, hidden_width)] * 2
    return pl.pallas_call(
        prepare_kernel,
        grid=(rows // block,),
        in_specs=[spec(low.shape), spec(hidden.shape)],
        out_specs=[spec(shape) for shape in shapes],
        out_shape=[jax.ShapeDtypeStruct(shape, jnp.bfloat16) for shape in shapes],
    )(low, hidden)


def finish_kernel(
    base,
    wide_low,
    wide_hidden,
    own_out,
    near_back,
    near_hidden,
    far_back,
    far_hidden,
    grad,
    in_grad,
    total,
):
    step = pl.program_id(0)
    block, width = base.shape
    parts, rank_width = SLOTS // BASE, grad.shape[0]
    for start in range(0, width, CHUNK):
        columns = slice(start, start + CHUNK)
        new = lax.dot_general(
            wide_low[...],
            base[:, columns],
            (((0,), (0,)), ((), ())),
            preferred_element_type=jnp.float32,
        )
        total[:, columns] = new + jnp.where(step == 0, 0.0, total[:, columns])
    wide_out = [own_out[:, at * width : (at + 1) * width] for at in range(parts)]
    halves = lax.dot_general(
        base[...],
        jnp.concatenate(wide_out, axis=0),
        (((1,), (1,)), ((), ())),
        preferred_element_type=jnp.float32,
    )
    back = halves[:, :rank_width]
    for at in range(1, parts):
        later = halves[:, at * rank_width : (at + 1) * rank_width]
        back = back + pltpu.roll(later, block - at, 0)
    whole = lax.broadcasted_iota(jnp.int32, back.shape, 0) % parts == 0
    back = jnp.where(whole, SCALE * back, 0.0).astype(jnp.bfloat16)
    new_in = lax.dot_general(
        back, wide_hidden[...], (((0,), (0,)), ((), ())), preferred_element_type=jnp.float32
    )


    @pl.when(step == 0)
    def _():
        start = new_in
        for back_rows, hidden_rows in ((near_back, near_hidden), (far_back, far_hidden)):
            start = start + lax.dot_general(
                back_rows[...],
                hidden_rows[...],
                (((0,), (0,)), ((), ())),
                preferred_element_type=jnp.float32,
            )
        in_grad[...] = start

    @pl.when(step > 0)
    def _():
        in_grad[...] += new_in

    @pl.when(step == pl.num_programs(0) - 1)
    def _():
        for at in range(parts):
            columns = slice(at * width, (at + 1) * width)
            rows = slice(at * rank_width, (at + 1) * rank_width)
            grad[:, columns] = total[rows, :]


def finish(base, wide_low, wide_hidden, *whole):
    rows, width = base.shape
    block = rows // 4
    own_out = whole[0]
    row_block = lambda array: pl.BlockSpec((block, array.shape[1]), lambda i: (i, 0))
    kept = lambda shape: pl.BlockSpec(shape, lambda i: (0, 0))
    out_shapes = (own_out.shape, (own_out.shape[0], wide_hidden.shape[1]))
    return pl.pallas_call(
        finish_kernel,
        grid=(rows // block,),
        in_specs=[row_block(x) for x in (base, wide_low, wide_hidden)]
        + [kept(x.shape) for x in whole],
        out_specs=[pl.BlockSpec(memory_space=pltpu.VMEM), kept(out_shapes[1])],
        out_shape=[
            pltpu.VMEM(out_shapes[0], jnp.float32),
            jax.ShapeDtypeStruct(out_shapes[1], jnp.float32),
        ],
        scratch_shapes=[pltpu.VMEM((wide_low.shape[1], width), jnp.float32)],
    )(base, wide_low, wide_hidden, *whole)


def exchange(block):
    return lax.all_to_all(block, AXES, split_axis=0, concat_axis=0, tiled=True)


def layer(
    tokens, cotangent, router_probs, routing, hot_marks, cap_counts, gate_up, adapter_in, adapter_out
):
    model_width = tokens.shape[1]
    experts = cap_counts.shape[0]
    n_expert = lax.axis_size("expert")
    half = n_expert // 2
    pairs = [(i, i ^ half) for i in range(n_expert)]
    own_index = lax.axis_index("dp") * n_expert + lax.axis_index("expert")
    own_in, own_out = adapter_in[0], adapter_out[0]

    partner_out = lax.ppermute(own_out, "expert", pairs)
    room = tokens.shape[0] * routing.shape[1] // experts
    tables = (
        routing.T,
        router_probs.T,
        hot_marks[None, :],
        cap_counts[None, :],
        own_index.reshape(1, 1),
    )
    first, second = pack(half, room, tables, (tokens, cotangent))
    first = exchange(first)
    own_index += jnp.isnan(first[0, 0, 0]).astype(jnp.int32)
    own_marked = lax.dynamic_index_in_dim(hot_marks, own_index, 0, keepdims=False) == 1
    second = exchange(second)

    inputs = first[:, :, :model_width].reshape(experts * SLOTS, model_width)
    gate_out = jnp.dot(inputs, gate_up[0, 0], preferred_element_type=jnp.float32)
    up_out = jnp.dot(inputs, gate_up[0, 1], preferred_element_type=jnp.float32)
    hidden = (jax.nn.silu(gate_out) * up_out).astype(jnp.bfloat16)
    low = (
        SCALE * jnp.einsum("nf,rf->nr", hidden, own_in, preferred_element_type=jnp.float32)
    ).astype(jnp.bfloat16)
    wide_low, wide_hidden, own_low, own_hidden, far_low, far_hidden = prepare(low, hidden)

    parts = SLOTS // EXTRA
    extra = first[:, :, model_width:].reshape(experts, EXTRA, parts, model_width // parts)
    extra = extra.reshape(experts * EXTRA, model_width)
    work_out = jnp.where(own_marked, own_out, partner_out)
    extra_back = (
        SCALE * jnp.einsum("nd,rd->nr", extra, work_out, preferred_element_type=jnp.float32)
    ).astype(jnp.bfloat16)
    swapped = lax.ppermute(jnp.where(own_marked, far_low, extra_back), "expert", pairs)
    extra_low = jnp.where(own_marked, own_low, swapped)
    extra_grad = jnp.einsum("nr,nd->rd", extra_low, extra, preferred_element_type=jnp.float32)
    returned = lax.ppermute(extra_grad.astype(jnp.bfloat16), "expert", pairs)
    grad, in_grad = finish(
        second.reshape(experts * SLOTS, BASE * model_width // SLOTS),
        wide_low,
        wide_hidden,
        own_out,
        extra_back,
        own_hidden,
        swapped,
        far_hidden,
    )
    out_grad = grad + jnp.where(own_marked, extra_grad + returned.astype(jnp.float32), 0.0)
    return in_grad[None], out_grad[None]


def solution(mesh):
    in_specs = (
        P(AXES, None),
        P(AXES, None),
        P(AXES, None),
        P(AXES, None),
        P(),
        P(),
        P(AXES, None, None, None),
        P(AXES, None, None),
        P(AXES, None, None),
    )
    out_specs = (P(AXES, None, None), P(AXES, None, None))
    return jax.shard_map(layer, mesh=mesh, in_specs=in_specs, out_specs=out_specs, check_vma=False)
```
